32 devices in a mesh: groups: 2 (over y), img: 4 (over z), tpl: 2 (over x), sub: 2 (over core).
Axes of the slice: x: 2, y: 2, z: 4, core: 2. Of those that a mesh axis runs over, the one named last changes fastest.
Arguments:
- images: bfloat16 [2048, 4096], P(('groups', 'img', 'tpl', 'sub')), parts along dimension 0, may hold values from -48 to 48
- templates: bfloat16 [4096, 4096], P(('groups', 'tpl', 'sub')), parts along dimension 0, may hold values from -1 to 1, as said below
- group_ids: int32 [2048], P(('groups', 'img')), parts along dimension 0, may hold values from 0 to 31
- group_ctf: float32 [64], P('groups'), parts along dimension 0, may hold values from 1 to 2
- group_prec: float32 [64], P('groups'), parts along dimension 0, may hold values from 1 to 3
- log_prior: float32 [256], P('groups'), parts along dimension 0, may hold values from -4.5 to 4.5
- class_mask: int32 [256], P('groups'), parts along dimension 0, may hold values from 0 to 1
Outputs:
- class_sums: float32 [4096, 4096], P(('groups', 'tpl', 'sub'), 'img'), parts along dimension 0
- evidence: float32 [2048], P(('groups', 'img', 'tpl', 'sub')), parts along dimension 0
The draws below stay inside these ranges and needn't reach their ends.
There are 2 independent parts, one for each index of `groups`. The reference program is written for one: setup_inputs(seed, part) draws one part's arguments, and reference() takes and returns one part's arrays. A program takes and returns all parts, laid end to end along the dimension named above; each array names one. Nothing has to cross between parts.
Inputs may be any that keep to these rules, and one draw needn't show every extreme that they name: `templates`: each row has unit length before rounding.
All inputs are finite; a program needn't handle non-finite values.
Results may differ from the reference program's by a relative error of at most 0.0028.
Values may be sent and summed in bfloat16 or wider, within the bound.
A program may use at most 64 MiB of HBM per device.

```python
import math
import jax
import jax.numpy as jnp
from jax import lax

PIX = 4096
CLASSES = 128
ROTS = 16
CTF_GROUPS = 32
IMG_DEV = 64
IMAGES = 1024
TEMPLATES = 2048
N_TPL = 2
N_SUB = 2


def tables_for(key):
    folded = jax.random.fold_in(key, 7)
    subkeys = jax.random.split(folded, 6)
    group_ids = jax.random.randint(subkeys[0], (IMAGES,), 0, CTF_GROUPS, dtype=jnp.int32)
    group_ctf = jnp.exp(jax.random.uniform(subkeys[1], (CTF_GROUPS,), jnp.float32, 0.0, math.log(2.0)))
    group_prec = jnp.exp(jax.random.uniform(subkeys[2], (CTF_GROUPS,), jnp.float32, 0.0, math.log(3.0)))
    log_prior = jnp.clip(0.7 * jax.random.normal(subkeys[3], (CLASSES,), jnp.float32), -4.5, 4.5)
    forced_class = jax.random.randint(subkeys[4], (), 0, CLASSES, dtype=jnp.int32)
    class_mask = (jax.random.randint(subkeys[5], (CLASSES,), 0, 4, dtype=jnp.int32) > 0).astype(jnp.int32)
    class_mask = jnp.where(jnp.arange(CLASSES, dtype=jnp.int32) == forced_class, 1, class_mask).astype(jnp.int32)
    return (group_ids, group_ctf, group_prec, log_prior, class_mask)


def templates_for(key):
    folded = jax.random.fold_in(key, 13)
    subkeys = jax.random.split(folded, 1)
    raw_field = jax.random.normal(subkeys[0], (TEMPLATES, PIX), jnp.float32)
    return raw_field / jnp.sqrt(jnp.sum(raw_field * raw_field, axis=1, keepdims=True))


def draw_templates(key, part):
    return templates_for(key).astype(jnp.bfloat16)


def draw_group_ids(key, part):
    return tables_for(key)[0]


def draw_group_ctf(key, part):
    return tables_for(key)[1]


def draw_group_prec(key, part):
    return tables_for(key)[2]


def draw_log_prior(key, part):
    return tables_for(key)[3]


def draw_class_mask(key, part):
    return tables_for(key)[4]


def draw_images(key, part):
    folded = jax.random.fold_in(key, 29)
    subkeys = jax.random.split(folded, 2)
    pixel_field = jax.random.normal(subkeys[1], (IMAGES, PIX), jnp.float32)
    return jnp.clip(pixel_field, -48.0, 48.0).astype(jnp.bfloat16)


def setup_inputs(seed: int = 0, part: int = 0) -> dict:
    seeds = jax.random.split(jax.random.key(seed), 8)
    part_keys = jax.random.split(jax.random.fold_in(seeds[7], part), 8)
    return {
        "images": draw_images(jax.random.fold_in(jax.random.fold_in(seeds[7], part), 71), part),
        "templates": draw_templates(jax.random.fold_in(jax.random.fold_in(seeds[7], part), 71), part),
        "group_ids": draw_group_ids(jax.random.fold_in(jax.random.fold_in(seeds[7], part), 71), part),
        "group_ctf": draw_group_ctf(jax.random.fold_in(jax.random.fold_in(seeds[7], part), 71), part),
        "group_prec": draw_group_prec(jax.random.fold_in(jax.random.fold_in(seeds[7], part), 71), part),
        "log_prior": draw_log_prior(jax.random.fold_in(jax.random.fold_in(seeds[7], part), 71), part),
        "class_mask": draw_class_mask(jax.random.fold_in(jax.random.fold_in(seeds[7], part), 71), part),
    }


masked_score = -1.0e30


def scored(raw_dots, tmpl_norm, scale_ctf, scale_prec, prior_rows, active):
    factor = (scale_prec * scale_ctf)[:, None]
    penalty = (0.5 * scale_prec * scale_ctf * scale_ctf)[:, None] * tmpl_norm[None, :]
    values = factor * raw_dots - penalty + prior_rows[None, :]
    return jnp.where(active[None, :], values, masked_score)


def reference(images, templates, group_ids, group_ctf, group_prec, log_prior, class_mask):
    tmpl_norm = jnp.sum(jnp.square(templates.astype(jnp.float32)), axis=1)
    prior_rows = jnp.repeat(log_prior, ROTS)
    active = jnp.repeat(class_mask, ROTS) > 0
    scale_ctf = group_ctf[group_ids]
    scale_prec = group_prec[group_ids]
    block_rows = IMG_DEV * N_TPL * N_SUB
    block_count = IMAGES // block_rows
    block_inputs = (images.reshape(block_count, block_rows, PIX), scale_ctf.reshape(block_count, block_rows), scale_prec.reshape(block_count, block_rows))

    def block_step(running, inputs):
        pixels_in, ctf_in, prec_in = inputs
        raw_dots = lax.dot_general(pixels_in, templates, (((1,), (1,)), ((), ())), preferred_element_type=jnp.float32)
        values = scored(raw_dots, tmpl_norm, ctf_in, prec_in, prior_rows, active)
        score_peak = jnp.max(values, axis=1)
        expo_terms = jnp.where(active[None, :], jnp.exp(values - score_peak[:, None]), 0.0)
        score_total = jnp.sum(expo_terms, axis=1)
        posterior = expo_terms / score_total[:, None]
        weight = (posterior * (prec_in * ctf_in)[:, None]).astype(jnp.bfloat16)
        running = running + lax.dot_general(weight, pixels_in, (((0,), (0,)), ((), ())), preferred_element_type=jnp.float32)
        return running, score_peak + jnp.log(score_total)

    class_sums, evidence = lax.scan(block_step, jnp.zeros((TEMPLATES, PIX), jnp.float32), block_inputs)
    return class_sums, evidence.reshape(IMAGES)
```

```python
import functools
import jax
import jax.numpy as jnp
from jax import lax
from jax.experimental import pallas as pl
from jax.experimental.pallas import tpu as pltpu
from jax.sharding import PartitionSpec as P

ROTS = 16
MASKED = -1e30
CHUNKS = 2
MESH = pl.DeviceIdType.MESH


def exchange_kernel(
    sizes, ids_ref, ctf_ref, prec_ref, prior_ref, mask_ref, images, templates,
    all_w, all_p, evid_ref,
    grid_buf, tmpl, tnorm, base, act, score, w_send, own_stat, stat,
    tmpl_sem, own_sem, a_send, a_recv, f_send, b_send, b_recv, g_send, s_send, s_recv,
    w_own, w_out, w_recv, p_own,
):
    Z, X, C, K, pb = sizes
    S = X * C
    g, z, x, c = [lax.axis_index(n) for n in ("groups", "img", "tpl", "sub")]
    s = x * C + c
    refs, nb = tnorm.shape
    classes = refs // ROTS

    def xc(dx, dc):
        return lax.rem(x + dx, X), lax.rem(c + dc, C)

    def dev(zz, xx, cc):
        return (g, zz, xx, cc)

    def zoff(d):
        return lax.rem(z + d, Z)

    peers = [(dx, dc) for dx in range(X) for dc in range(C) if dx or dc]

    barrier = pltpu.get_barrier_semaphore()
    for dx, dc in peers:
        pl.semaphore_signal(barrier, inc=1, device_id=dev(z, *xc(dx, dc)), device_id_type=MESH)
    for d in range(1, Z):
        pl.semaphore_signal(barrier, inc=1, device_id=dev(zoff(d), x, c), device_id_type=MESH)

    started = []

    def local(src, dst, sem):
        cp = pltpu.make_async_copy(src, dst, sem)
        cp.start()
        return cp

    def remote(src, dst, send, recv, to):
        cp = pltpu.make_async_remote_copy(
            src_ref=src, dst_ref=dst, send_sem=send, recv_sem=recv, device_id=to, device_id_type=MESH
        )
        cp.start()
        started.append(cp)

    def arrive(dst, sem):
        pltpu.make_async_copy(dst, dst, sem).wait()

    tmpl_copy = local(templates, tmpl, tmpl_sem)
    own_copies = [local(images.at[k], grid_buf.at[k, s], own_sem.at[k]) for k in range(K)]

    pl.semaphore_wait(barrier, S - 1 + Z - 1)

    def send_a(k):
        for dx in range(1, X):
            xx, cc = xc(dx, 0)
            remote(images.at[k], grid_buf.at[k, s], a_send.at[k, dx - 1], a_recv.at[k, s], dev(z, xx, cc))
        for dc in range(1, C):
            xx, cc = xc(0, dc)
            remote(images.at[k], grid_buf.at[k, s], a_send.at[k, X - 1 + dc - 1], a_recv.at[k, s], dev(z, xx, cc))

    send_a(0)
    for d in range(1, Z):
        zz = zoff(d)
        cols = pl.ds(pl.multiple_of(zz * pb, pb), pb)
        remote(images.at[:, :, cols], all_p.at[:, z, s], b_send.at[d - 1], b_recv.at[z, s], dev(zz, x, c))
    for k in range(1, K):
        send_a(k)

    first = s * classes
    for i in range(classes):
        rows = pl.ds(i * ROTS, ROTS)
        base[rows, :] = jnp.full((ROTS, nb), prior_ref[first + i], jnp.float32)
        act[rows, :] = jnp.full((ROTS, nb), mask_ref[first + i], jnp.int32).astype(jnp.float32)

    tmpl_copy.wait()

    @pl.loop(0, refs // 16)
    def _(i):
        rows = pl.ds(pl.multiple_of(i * 16, 16), 16)
        t = tmpl[rows, :].astype(jnp.float32)
        tnorm[rows, :] = jnp.broadcast_to(jnp.sum(t * t, axis=1, keepdims=True), (16, nb))

    def scales(k):
        ids = ids_ref[k]
        ctf = jnp.zeros_like(ids, dtype=jnp.float32)
        prec = ctf
        for i in range(ctf_ref.shape[0]):
            hit = ids == i
            ctf = jnp.where(hit, ctf_ref[i], ctf)
            prec = jnp.where(hit, prec_ref[i], prec)
        return ctf, prec

    p_copies = []

    def gather(k):
        own_copies[k].wait()
        for dx in range(1, X):
            xx, _ = xc(dx, 0)
            slot = xx * C + c
            arrive(grid_buf.at[k, slot], a_recv.at[k, slot])
            for dc in range(1, C):
                _, cc = xc(0, dc)
                remote(grid_buf.at[k, slot], grid_buf.at[k, slot], f_send.at[k, dx - 1, dc - 1], a_recv.at[k, slot], dev(z, x, cc))
        for dx in range(X):
            for dc in range(1, C):
                xx, cc = xc(dx, dc)
                slot = xx * C + cc
                arrive(grid_buf.at[k, slot], a_recv.at[k, slot])

    def scores(k):
        pix = grid_buf[k].reshape(nb, grid_buf.shape[3])
        raw = lax.dot_general(tmpl[...], pix, (((1,), (1,)), ((), ())), preferred_element_type=jnp.float32)
        ctf, prec = scales(k)
        values = (prec * ctf) * raw - (0.5 * prec * ctf * ctf) * tnorm[...] + base[...]
        values = jnp.where(act[...] > 0.0, values, MASKED)
        score[k] = values
        peak = jnp.max(values, axis=0, keepdims=True)
        total = jnp.sum(jnp.where(act[...] > 0.0, jnp.exp(values - peak), 0.0), axis=0, keepdims=True)
        row = lax.broadcasted_iota(jnp.int32, (8, nb), 0)
        own_stat[k] = jnp.where(row == 0, peak, total)
        for i, (dx, dc) in enumerate(peers):
            xx, cc = xc(dx, dc)
            remote(own_stat.at[k], stat.at[k, s], s_send.at[k, i], s_recv.at[k, s], dev(z, xx, cc))
        cols = pl.ds(pl.multiple_of(z * pb, pb), pb)
        p_copies.append(local(grid_buf.at[k, :, :, cols], all_p.at[k, z], p_own.at[k]))

    def w_block(ref, k, zz):
        return ref.at[:, pl.ds(pl.multiple_of((k * Z + zz) * nb, nb), nb)]

    def w_go(src, k, zz, right):
        step = 1 if right else -1
        return pltpu.make_async_remote_copy(
            src_ref=src, dst_ref=w_block(all_w, k, zz), send_sem=w_out.at[0 if right else 1, k, zz],
            recv_sem=w_recv.at[k, zz], device_id=dev(lax.rem(z + step + Z, Z), x, c), device_id_type=MESH,
        )

    w_copies = []

    def weights(k):
        parts = [(own_stat[k][0:1], own_stat[k][1:2])]
        for dx, dc in peers:
            xx, cc = xc(dx, dc)
            slot = xx * C + cc
            arrive(stat.at[k, slot], s_recv.at[k, slot])
            got = stat[k, slot]
            parts.append((got[0:1], got[1:2]))
        peak = functools.reduce(jnp.maximum, [p for p, _ in parts])
        total = functools.reduce(jnp.add, [t * jnp.exp(p - peak) for p, t in parts])
        evid_ref[k] = peak + jnp.log(total)
        ctf, prec = scales(k)
        post = jnp.where(act[...] > 0.0, jnp.exp(score[k] - peak), 0.0) / total
        w_send[k] = (post * (prec * ctf)).astype(jnp.bfloat16)

        @pl.when(z < Z - 1)
        def _():
            w_go(w_send.at[k], k, z, True).start()

        @pl.when(z > 0)
        def _():
            w_go(w_send.at[k], k, z, False).start()

        w_copies.append(local(w_send.at[k], w_block(all_w, k, z), w_own.at[k]))

    gather(0)
    scores(0)
    for k in range(1, K):
        gather(k)
        weights(k - 1)
        scores(k)
    weights(K - 1)

    for d in range(1, Z):
        zz = zoff(d)
        blk = all_p.at[:, zz, s]
        arrive(blk, b_recv.at[zz, s])
        for dx in range(1, X):
            xx, cc = xc(dx, 0)
            remote(blk, blk, g_send.at[d - 1, dx - 1, 0], b_recv.at[zz, s], dev(z, xx, cc))
        for dc in range(1, C):
            xx, cc = xc(0, dc)
            remote(blk, blk, g_send.at[d - 1, X - 1, dc - 1], b_recv.at[zz, s], dev(z, xx, cc))

    for d in range(1, Z):
        for k in range(K):
            @pl.when(z - d >= 0)
            def _():
                src = z - d
                arrive(w_block(all_w, k, src), w_recv.at[k, src])

                @pl.when(z < Z - 1)
                def _():
                    w_go(w_block(all_w, k, src), k, src, True).start()

            @pl.when(z + d < Z)
            def _():
                src = z + d
                arrive(w_block(all_w, k, src), w_recv.at[k, src])

                @pl.when(z > 0)
                def _():
                    w_go(w_block(all_w, k, src), k, src, False).start()
        zz = zoff(d)
        for dx in range(1, X):
            xx, _ = xc(dx, 0)
            blk = all_p.at[:, zz, xx * C + c]
            arrive(blk, b_recv.at[zz, xx * C + c])
            for dc in range(1, C):
                _, cc = xc(0, dc)
                remote(blk, blk, g_send.at[d - 1, dx - 1, dc], b_recv.at[zz, xx * C + c], dev(z, x, cc))

    for d in range(1, Z):
        zz = zoff(d)
        for dx in range(X):
            for dc in range(1, C):
                xx, cc = xc(dx, dc)
                arrive(all_p.at[:, zz, xx * C + cc], b_recv.at[zz, xx * C + cc])
    for cp in started:
        cp.wait_send()
    for k in range(K):
        w_copies[k].wait()
        p_copies[k].wait()
        for d in range(Z):
            @pl.when((z - d >= 0) & (z < Z - 1))
            def _():
                w_go(w_send.at[k], k, z - d, True).wait_send()

            @pl.when((z + d < Z) & (z > 0))
            def _():
                w_go(w_send.at[k], k, z + d, False).wait_send()


def exchange(mesh, images, templates, group_ids, group_ctf, group_prec, log_prior, class_mask):
    Z, X, C, K = mesh.shape["img"], mesh.shape["tpl"], mesh.shape["sub"], CHUNKS
    S = X * C
    rows, pix = images.shape
    refs = templates.shape[0]
    r = rows // K
    nb = S * r
    pb = pix // Z
    ids = group_ids.reshape(S, K, r).transpose(1, 0, 2).reshape(K, 1, nb)
    smem = pl.BlockSpec(memory_space=pltpu.SMEM)
    vmem = pl.BlockSpec(memory_space=pltpu.VMEM)
    anyw = pl.BlockSpec(memory_space=pl.ANY)
    dma = pltpu.SemaphoreType.DMA
    f32, bf16 = jnp.float32, jnp.bfloat16
    all_w, all_p, evid = pl.pallas_call(
        functools.partial(exchange_kernel, (Z, X, C, K, pb)),
        out_shape=(
            jax.ShapeDtypeStruct((refs, K * Z * nb), bf16),
            jax.ShapeDtypeStruct((K, Z, S, r, pb), bf16),
            jax.ShapeDtypeStruct((K, 1, nb), f32),
        ),
        in_specs=[vmem, smem, smem, smem, smem, anyw, anyw],
        out_specs=(anyw, anyw, vmem),
        scratch_shapes=[
            pltpu.VMEM((K, S, r, pix), bf16),
            pltpu.VMEM((refs, pix), bf16),
            pltpu.VMEM((refs, nb), f32),
            pltpu.VMEM((refs, nb), f32),
            pltpu.VMEM((refs, nb), f32),
            pltpu.VMEM((K, refs, nb), f32),
            pltpu.VMEM((K, refs, nb), bf16),
            pltpu.VMEM((K, 8, nb), f32),
            pltpu.VMEM((K, S, 8, nb), f32),
            dma(()), dma((K,)), dma((K, S)), dma((K, S)), dma((K, max(X - 1, 1), max(C - 1, 1))),
            dma((max(Z - 1, 1),)), dma((Z, S)), dma((max(Z - 1, 1), X, C)), dma((K, max(S - 1, 1))), dma((K, S)),
            dma((K,)), dma((2, K, Z)), dma((K, Z)), dma((K,)),
        ],
        compiler_params=pltpu.CompilerParams(
            collective_id=0, has_side_effects=True, vmem_limit_bytes=56 * 1024 * 1024
        ),
    )(ids, group_ctf, group_prec, log_prior, class_mask, images.reshape(K, r, pix), templates)
    class_sums = lax.dot_general(
        all_w, all_p.reshape(K * Z * nb, pb), (((1,), (0,)), ((), ())), preferred_element_type=f32
    )
    slot = lax.axis_index(("tpl", "sub"))
    own = lax.dynamic_slice_in_dim(evid.reshape(K, S, r), slot, 1, axis=1)
    return class_sums, own.reshape(rows)


def solution(mesh):
    placed = (
        P(("groups", "img", "tpl", "sub"), None),
        P(("groups", "tpl", "sub"), None),
        P(("groups", "img")),
        P("groups"),
        P("groups"),
        P("groups"),
        P("groups"),
    )
    return jax.shard_map(
        functools.partial(exchange, mesh),
        mesh=mesh,
        in_specs=placed,
        out_specs=(P(("groups", "tpl", "sub"), "img"), P(("groups", "img", "tpl", "sub"))),
        check_vma=False,
    )
```

```python
import functools
import jax
import jax.numpy as jnp
from jax import lax
from jax.experimental import pallas as pl
from jax.experimental.pallas import tpu as pltpu
from jax.sharding import PartitionSpec as P

ROTS = 16
MASKED = -1e30
CHUNKS = 2
MESH = pl.DeviceIdType.MESH


def exchange_kernel(
    sizes, ids_ref, ctf_ref, prec_ref, prior_ref, mask_ref, images, templates,
    sums_ref, evid_ref,
    grid_buf, tmpl, tnorm, base, act, score, all_w, all_p, own_stat, stat,
    tmpl_sem, own_sem, a_send, a_recv, f_send, b_send, b_recv, g_send, s_send, s_recv,
    w_out, w_recv, p_own,
):
    Z, X, C, K, H = sizes
    S = X * C
    g, z, x, c = [lax.axis_index(n) for n in ("groups", "img", "tpl", "sub")]
    s = x * C + c
    refs, nb = tnorm.shape
    classes = refs // ROTS
    r, pix = grid_buf.shape[2:]
    pb = pix // Z
    h_rows = r // H

    def xc(dx, dc):
        return lax.rem(x + dx, X), lax.rem(c + dc, C)

    def dev(zz, xx, cc):
        return (g, zz, xx, cc)

    def zoff(d):
        return lax.rem(z + d, Z)

    peers = [(dx, dc) for dx in range(X) for dc in range(C) if dx or dc]

    barrier = pltpu.get_barrier_semaphore()
    for dx, dc in peers:
        pl.semaphore_signal(barrier, inc=1, device_id=dev(z, *xc(dx, dc)), device_id_type=MESH)
    for d in range(1, Z):
        pl.semaphore_signal(barrier, inc=1, device_id=dev(zoff(d), x, c), device_id_type=MESH)

    started = []

    def local(src, dst, sem):
        cp = pltpu.make_async_copy(src, dst, sem)
        cp.start()
        return cp

    def remote(src, dst, send, recv, to):
        cp = pltpu.make_async_remote_copy(
            src_ref=src, dst_ref=dst, send_sem=send, recv_sem=recv, device_id=to, device_id_type=MESH
        )
        cp.start()
        started.append(cp)

    def arrive(dst, sem):
        pltpu.make_async_copy(dst, dst, sem).wait()

    tmpl_copy = local(templates, tmpl, tmpl_sem)
    own_copies = [local(images.at[k], grid_buf.at[k, s], own_sem.at[k]) for k in range(K)]

    pl.semaphore_wait(barrier, S - 1 + Z - 1)

    def piece(k, h, slot):
        return grid_buf.at[k, slot, pl.ds(h * h_rows, h_rows), :]

    def send_a(k, h):
        src = images.at[k, pl.ds(h * h_rows, h_rows), :]
        for dx in range(1, X):
            xx, cc = xc(dx, 0)
            remote(src, piece(k, h, s), a_send.at[k, h, dx - 1], a_recv.at[k, h, s], dev(z, xx, cc))
        for dc in range(1, C):
            xx, cc = xc(0, dc)
            remote(src, piece(k, h, s), a_send.at[k, h, X - 1 + dc - 1], a_recv.at[k, h, s], dev(z, xx, cc))

    order = [(k, h) for k in range(K) for h in range(H)]
    early = [kh for kh in order if kh[0] == 0 or kh[1] < H - 1]
    for k, h in early[:H]:
        send_a(k, h)
    for d in range(1, Z):
        zz = zoff(d)
        cols = pl.ds(pl.multiple_of(zz * pb, pb), pb)
        remote(images.at[:, :, cols], all_p.at[z, :, s], b_send.at[d - 1], b_recv.at[z, s], dev(zz, x, c))
    for k, h in early[H:]:
        send_a(k, h)

    first = s * classes
    for i in range(classes):
        rows = pl.ds(i * ROTS, ROTS)
        base[rows, :] = jnp.full((ROTS, nb), prior_ref[first + i], jnp.float32)
        act[rows, :] = jnp.full((ROTS, nb), mask_ref[first + i], jnp.int32).astype(jnp.float32)

    tmpl_copy.wait()

    @pl.loop(0, refs // 16)
    def _(i):
        rows = pl.ds(pl.multiple_of(i * 16, 16), 16)
        t = tmpl[rows, :].astype(jnp.float32)
        tnorm[rows, :] = jnp.broadcast_to(jnp.sum(t * t, axis=1, keepdims=True), (16, nb))

    all_ids = ids_ref[...]
    all_ctf = jnp.zeros(all_ids.shape, jnp.float32)
    all_prec = all_ctf
    for i in range(ctf_ref.shape[0]):
        hit = all_ids == i
        all_ctf = jnp.where(hit, ctf_ref[i], all_ctf)
        all_prec = jnp.where(hit, prec_ref[i], all_prec)

    def chunk(row, k):
        return jnp.concatenate([row[:, q * K * r + k * r : q * K * r + (k + 1) * r] for q in range(S)], axis=1)

    ctfs = [chunk(all_ctf, k) for k in range(K)]
    precs = [chunk(all_prec, k) for k in range(K)]

    def gather(k):
        own_copies[k].wait()
        for h in range(H):
            for dx in range(1, X):
                xx, _ = xc(dx, 0)
                slot = xx * C + c
                arrive(piece(k, h, slot), a_recv.at[k, h, slot])
                for dc in range(1, C):
                    _, cc = xc(0, dc)
                    remote(piece(k, h, slot), piece(k, h, slot), f_send.at[k, h, dx - 1, dc - 1], a_recv.at[k, h, slot], dev(z, x, cc))
        for h in range(H):
            for dx in range(X):
                for dc in range(1, C):
                    xx, cc = xc(dx, dc)
                    slot = xx * C + cc
                    arrive(piece(k, h, slot), a_recv.at[k, h, slot])

    p_copies = []

    def scores(k):
        pixels = grid_buf[k].reshape(nb, pix)
        raw = lax.dot_general(tmpl[...], pixels, (((1,), (1,)), ((), ())), preferred_element_type=jnp.float32)
        ctf, prec = ctfs[k], precs[k]
        values = (prec * ctf) * raw - (0.5 * prec * ctf * ctf) * tnorm[...] + base[...]
        values = jnp.where(act[...] > 0.0, values, MASKED)
        score[k] = values
        peak = jnp.max(values, axis=0, keepdims=True)
        total = jnp.sum(jnp.where(act[...] > 0.0, jnp.exp(values - peak), 0.0), axis=0, keepdims=True)
        row = lax.broadcasted_iota(jnp.int32, (8, nb), 0)
        own_stat[k] = jnp.where(row == 0, peak, total)
        for i, (dx, dc) in enumerate(peers):
            xx, cc = xc(dx, dc)
            remote(own_stat.at[k], stat.at[k, s], s_send.at[k, i], s_recv.at[k, s], dev(z, xx, cc))
        cols = pl.ds(pl.multiple_of(z * pb, pb), pb)
        p_copies.append(local(grid_buf.at[k, :, :, cols], all_p.at[z, k], p_own.at[k]))

    def w_go(k, zz, right):
        step = 1 if right else -1
        return pltpu.make_async_remote_copy(
            src_ref=all_w.at[k, zz], dst_ref=all_w.at[k, zz], send_sem=w_out.at[0 if right else 1, k, zz],
            recv_sem=w_recv.at[k, zz], device_id=dev(lax.rem(z + step + Z, Z), x, c), device_id_type=MESH,
        )

    def weights(k):
        parts = [(own_stat[k][0:1], own_stat[k][1:2])]
        for dx, dc in peers:
            xx, cc = xc(dx, dc)
            slot = xx * C + cc
            arrive(stat.at[k, slot], s_recv.at[k, slot])
            got = stat[k, slot]
            parts.append((got[0:1], got[1:2]))
        peak = functools.reduce(jnp.maximum, [p for p, _ in parts])
        total = functools.reduce(jnp.add, [t * jnp.exp(p - peak) for p, t in parts])
        evid = peak + jnp.log(total)
        mine = evid[:, 0:r]
        for q in range(1, S):
            mine = jnp.where(s == q, evid[:, q * r : (q + 1) * r], mine)
        evid_ref[:, k * r : (k + 1) * r] = mine
        post = jnp.where(act[...] > 0.0, jnp.exp(score[k] - peak), 0.0) / total
        all_w[k, z] = (post * (precs[k] * ctfs[k])).astype(jnp.bfloat16)

        @pl.when(z < Z - 1)
        def _():
            w_go(k, z, True).start()

        @pl.when(z > 0)
        def _():
            w_go(k, z, False).start()

    gather(0)
    scores(0)
    for k in range(1, K):
        for h in range(H):
            if (k, h) not in early:
                send_a(k, h)
    for k in range(1, K):
        gather(k)
        weights(k - 1)
        scores(k)

    def b_block(zz, slot):
        return all_p.at[zz, :, slot]

    def b_forward(zz):
        out = []
        for dx in range(1, X):
            xx, cc = xc(dx, 0)
            out.append((g_send.at[zz, dx - 1, 0], dev(z, xx, cc)))
        for dc in range(1, C):
            xx, cc = xc(0, dc)
            out.append((g_send.at[zz, X - 1, dc - 1], dev(z, xx, cc)))
        return [
            pltpu.make_async_remote_copy(
                src_ref=b_block(zz, s), dst_ref=b_block(zz, s), send_sem=sem, recv_sem=b_recv.at[zz, s],
                device_id=to, device_id_type=MESH,
            )
            for sem, to in out
        ]

    def b_second(zz):
        out = []
        for dx in range(1, X):
            xx, _ = xc(dx, 0)
            slot = xx * C + c
            for dc in range(1, C):
                _, cc = xc(0, dc)
                out.append(pltpu.make_async_remote_copy(
                    src_ref=b_block(zz, slot), dst_ref=b_block(zz, slot), send_sem=g_send.at[zz, dx - 1, dc],
                    recv_sem=b_recv.at[zz, slot], device_id=dev(z, x, cc), device_id_type=MESH,
                ))
        return out

    def both(d, fn):
        @pl.when(z - d >= 0)
        def _():
            fn(z - d, True)

        @pl.when(z + d < Z)
        def _():
            fn(z + d, False)

    def b_start(zz, right):
        arrive(b_block(zz, s), b_recv.at[zz, s])
        for cp in b_forward(zz):
            cp.start()

    @pl.loop(1, Z)
    def _(d):
        both(d, b_start)

    weights(K - 1)

    def product(zz):
        w = jnp.concatenate([all_w[k, zz] for k in range(K)], axis=1)
        p = all_p[zz].reshape(K * nb, pb)
        return jnp.dot(w, p, preferred_element_type=jnp.float32)

    for cp in p_copies:
        cp.wait()
    sums_ref[...] = product(z)

    def w_step(src, right):
        for k in range(K):
            arrive(all_w.at[k, src], w_recv.at[k, src])

            @pl.when((z < Z - 1) if right else (z > 0))
            def _():
                w_go(k, src, right).start()

    def p_step(src, right):
        for dx in range(1, X):
            xx, _ = xc(dx, 0)
            arrive(b_block(src, xx * C + c), b_recv.at[src, xx * C + c])
        for cp in b_second(src):
            cp.start()

    def add_step(src, right):
        for dx in range(X):
            for dc in range(1, C):
                xx, cc = xc(dx, dc)
                arrive(b_block(src, xx * C + cc), b_recv.at[src, xx * C + cc])
        sums_ref[...] += product(src)

    @pl.loop(1, Z + 1)
    def _(d):
        both(d, w_step)
        both(d, p_step)

        @pl.when(d > 1)
        def _():
            both(d - 1, add_step)

    for cp in started:
        cp.wait_send()

    def end_step(src, right):
        for cp in b_forward(src) + b_second(src):
            cp.wait_send()

    @pl.loop(1, Z)
    def _(d):
        both(d, end_step)

    for k in range(K):
        @pl.loop(0, Z)
        def _(d):
            @pl.when((z - d >= 0) & (z < Z - 1))
            def _():
                w_go(k, z - d, True).wait_send()

            @pl.when((z + d < Z) & (z > 0))
            def _():
                w_go(k, z + d, False).wait_send()


def exchange(mesh, images, templates, group_ids, group_ctf, group_prec, log_prior, class_mask):
    Z, X, C, K = mesh.shape["img"], mesh.shape["tpl"], mesh.shape["sub"], CHUNKS
    S = X * C
    rows, pix = images.shape
    refs = templates.shape[0]
    r = rows // K
    nb = S * r
    pb = pix // Z
    H = 2 if r % 32 == 0 else 1
    smem = pl.BlockSpec(memory_space=pltpu.SMEM)
    vmem = pl.BlockSpec(memory_space=pltpu.VMEM)
    anyw = pl.BlockSpec(memory_space=pl.ANY)
    dma = pltpu.SemaphoreType.DMA
    f32, bf16 = jnp.float32, jnp.bfloat16
    class_sums, evid = pl.pallas_call(
        functools.partial(exchange_kernel, (Z, X, C, K, H)),
        out_shape=(
            jax.ShapeDtypeStruct((refs, pb), f32),
            jax.ShapeDtypeStruct((1, rows), f32),
        ),
        in_specs=[vmem, smem, smem, smem, smem, anyw, anyw],
        out_specs=(vmem, vmem),
        scratch_shapes=[
            pltpu.VMEM((K, S, r, pix), bf16),
            pltpu.VMEM((refs, pix), bf16),
            pltpu.VMEM((refs, nb), f32),
            pltpu.VMEM((refs, nb), f32),
            pltpu.VMEM((refs, nb), f32),
            pltpu.VMEM((K, refs, nb), f32),
            pltpu.VMEM((K, Z, refs, nb), bf16),
            pltpu.VMEM((Z, K, S, r, pb), bf16),
            pltpu.VMEM((K, 8, nb), f32),
            pltpu.VMEM((K, S, 8, nb), f32),
            dma(()), dma((K,)), dma((K, H, S)), dma((K, H, S)), dma((K, H, max(X - 1, 1), max(C - 1, 1))),
            dma((max(Z - 1, 1),)), dma((Z, S)), dma((Z, X, C)), dma((K, max(S - 1, 1))), dma((K, S)),
            dma((2, K, Z)), dma((K, Z)), dma((K,)),
        ],
        compiler_params=pltpu.CompilerParams(
            collective_id=0, has_side_effects=True, vmem_limit_bytes=56 * 1024 * 1024
        ),
    )(group_ids.reshape(1, S * rows), group_ctf, group_prec, log_prior, class_mask, images.reshape(K, r, pix), templates)
    return class_sums, evid.reshape(rows)


def solution(mesh):
    placed = (
        P(("groups", "img", "tpl", "sub"), None),
        P(("groups", "tpl", "sub"), None),
        P(("groups", "img")),
        P("groups"),
        P("groups"),
        P("groups"),
        P("groups"),
    )
    return jax.shard_map(
        functools.partial(exchange, mesh),
        mesh=mesh,
        in_specs=placed,
        out_specs=(P(("groups", "tpl", "sub"), "img"), P(("groups", "img", "tpl", "sub"))),
        check_vma=False,
    )
```

```python
import functools
import jax
import jax.numpy as jnp
from jax import lax
from jax.experimental import pallas as pl
from jax.experimental.pallas import tpu as pltpu
from jax.sharding import PartitionSpec as P

ROTS = 16
MASKED = -1e30
CHUNKS = 2
MESH = pl.DeviceIdType.MESH


def exchange_kernel(
    sizes, ids_in, ctf_in, prec_in, prior_in, mask_in, images, templates,
    sums_ref, evid_ref,
    ids_ref, ctf_ref, prec_ref, prior_ref, mask_ref, grid_buf, tmpl, tnorm, base, act, score, all_w, all_p, own_stat, stat,
    tmpl_sem, own_sem, a_send, a_recv, f_send, b_send, b_recv, g_send, s_send, s_recv,
    w_out, w_recv, p_own, in_sem,
):
    Z, X, C, K, H = sizes
    S = X * C
    g, z, x, c = [lax.axis_index(n) for n in ("groups", "img", "tpl", "sub")]
    s = x * C + c
    refs, nb = tnorm.shape
    classes = refs // ROTS
    r, pix = grid_buf.shape[2:]
    pb = pix // Z
    h_rows = r // H

    def xc(dx, dc):
        return lax.rem(x + dx, X), lax.rem(c + dc, C)

    def dev(zz, xx, cc):
        return (g, zz, xx, cc)

    def zoff(d):
        return lax.rem(z + d, Z)

    peers = [(dx, dc) for dx in range(X) for dc in range(C) if dx or dc]

    barrier = pltpu.get_barrier_semaphore()
    for dx, dc in peers:
        pl.semaphore_signal(barrier, inc=1, device_id=dev(z, *xc(dx, dc)), device_id_type=MESH)
    for d in range(1, Z):
        pl.semaphore_signal(barrier, inc=1, device_id=dev(zoff(d), x, c), device_id_type=MESH)

    started = []

    def local(src, dst, sem):
        cp = pltpu.make_async_copy(src, dst, sem)
        cp.start()
        return cp

    def remote(src, dst, send, recv, to):
        cp = pltpu.make_async_remote_copy(
            src_ref=src, dst_ref=dst, send_sem=send, recv_sem=recv, device_id=to, device_id_type=MESH
        )
        cp.start()
        started.append(cp)

    def arrive(dst, sem):
        pltpu.make_async_copy(dst, dst, sem).wait()

    small = [
        local(src, dst, in_sem.at[i])
        for i, (src, dst) in enumerate((
            (ids_in, ids_ref), (ctf_in, ctf_ref), (prec_in, prec_ref), (prior_in, prior_ref), (mask_in, mask_ref),
        ))
    ]
    tmpl_copy = local(templates, tmpl, tmpl_sem)
    own_copies = [local(images.at[k], grid_buf.at[k, s], own_sem.at[k]) for k in range(K)]

    pl.semaphore_wait(barrier, S - 1 + Z - 1)

    def piece(k, h, slot):
        return grid_buf.at[k, slot, pl.ds(h * h_rows, h_rows), :]

    def send_a(k, h):
        src = images.at[k, pl.ds(h * h_rows, h_rows), :]
        for dx in range(1, X):
            xx, cc = xc(dx, 0)
            remote(src, piece(k, h, s), a_send.at[k, h, dx - 1], a_recv.at[k, h, s], dev(z, xx, cc))
        for dc in range(1, C):
            xx, cc = xc(0, dc)
            remote(src, piece(k, h, s), a_send.at[k, h, X - 1 + dc - 1], a_recv.at[k, h, s], dev(z, xx, cc))

    order = [(k, h) for k in range(K) for h in range(H)]
    early = [(k, h) for k, h in order if k == 0 or h < H - 1]
    for k, h in early[:H]:
        send_a(k, h)
    for d in range(1, Z):
        zz = zoff(d)
        cols = pl.ds(pl.multiple_of(zz * pb, pb), pb)
        remote(images.at[:, :, cols], all_p.at[z, :, s], b_send.at[d - 1], b_recv.at[z, s], dev(zz, x, c))
    for k, h in early[H:]:
        send_a(k, h)

    for cp in small:
        cp.wait()
    first = s * classes
    for i in range(classes):
        rows = pl.ds(i * ROTS, ROTS)
        base[rows, :] = jnp.full((ROTS, nb), prior_ref[first + i], jnp.float32)
        act[rows, :] = jnp.full((ROTS, nb), mask_ref[first + i], jnp.int32).astype(jnp.float32)

    tmpl_copy.wait()

    @pl.loop(0, refs // 16)
    def _(i):
        rows = pl.ds(pl.multiple_of(i * 16, 16), 16)
        t = tmpl[rows, :].astype(jnp.float32)
        tnorm[rows, :] = jnp.broadcast_to(jnp.sum(t * t, axis=1, keepdims=True), (16, nb))

    all_ids = ids_ref[...]
    all_ctf = jnp.zeros(all_ids.shape, jnp.float32)
    all_prec = all_ctf
    for i in range(ctf_ref.shape[0]):
        hit = all_ids == i
        all_ctf = jnp.where(hit, ctf_ref[i], all_ctf)
        all_prec = jnp.where(hit, prec_ref[i], all_prec)

    def chunk(row, k):
        return jnp.concatenate([row[:, q * K * r + k * r : q * K * r + (k + 1) * r] for q in range(S)], axis=1)

    ctfs = [chunk(all_ctf, k) for k in range(K)]
    precs = [chunk(all_prec, k) for k in range(K)]

    def gather(k, h):
        for dx in range(1, X):
            xx, _ = xc(dx, 0)
            slot = xx * C + c
            arrive(piece(k, h, slot), a_recv.at[k, h, slot])
            for dc in range(1, C):
                _, cc = xc(0, dc)
                remote(piece(k, h, slot), piece(k, h, slot), f_send.at[k, h, dx - 1, dc - 1], a_recv.at[k, h, slot], dev(z, x, cc))

    def gathered(k):
        own_copies[k].wait()
        for h in range(H):
            for dx in range(X):
                for dc in range(1, C):
                    xx, cc = xc(dx, dc)
                    slot = xx * C + cc
                    arrive(piece(k, h, slot), a_recv.at[k, h, slot])

    p_copies = []

    def scores(k):
        pixels = grid_buf[k].reshape(nb, pix)
        raw = lax.dot_general(tmpl[...], pixels, (((1,), (1,)), ((), ())), preferred_element_type=jnp.float32)
        ctf, prec = ctfs[k], precs[k]
        values = (prec * ctf) * raw - (0.5 * prec * ctf * ctf) * tnorm[...] + base[...]
        values = jnp.where(act[...] > 0.0, values, MASKED)
        score[k] = values
        peak = jnp.max(values, axis=0, keepdims=True)
        total = jnp.sum(jnp.where(act[...] > 0.0, jnp.exp(values - peak), 0.0), axis=0, keepdims=True)
        row = lax.broadcasted_iota(jnp.int32, (8, nb), 0)
        own_stat[k] = jnp.where(row == 0, peak, total)
        for i, (dx, dc) in enumerate(peers):
            xx, cc = xc(dx, dc)
            remote(own_stat.at[k], stat.at[k, s], s_send.at[k, i], s_recv.at[k, s], dev(z, xx, cc))
        cols = pl.ds(pl.multiple_of(z * pb, pb), pb)
        p_copies.append(local(grid_buf.at[k, :, :, cols], all_p.at[z, k], p_own.at[k]))

    def w_go(k, zz, right):
        step = 1 if right else -1
        return pltpu.make_async_remote_copy(
            src_ref=all_w.at[k, zz], dst_ref=all_w.at[k, zz], send_sem=w_out.at[0 if right else 1, k, zz],
            recv_sem=w_recv.at[k, zz], device_id=dev(lax.rem(z + step + Z, Z), x, c), device_id_type=MESH,
        )

    def weights(k):
        parts = [(own_stat[k][0:1], own_stat[k][1:2])]
        for dx, dc in peers:
            xx, cc = xc(dx, dc)
            slot = xx * C + cc
            arrive(stat.at[k, slot], s_recv.at[k, slot])
            got = stat[k, slot]
            parts.append((got[0:1], got[1:2]))
        peak = functools.reduce(jnp.maximum, [p for p, _ in parts])
        total = functools.reduce(jnp.add, [t * jnp.exp(p - peak) for p, t in parts])
        evid = peak + jnp.log(total)
        mine = evid[:, 0:r]
        for q in range(1, S):
            mine = jnp.where(s == q, evid[:, q * r : (q + 1) * r], mine)
        evid_ref[:, k * r : (k + 1) * r] = mine
        post = jnp.where(act[...] > 0.0, jnp.exp(score[k] - peak), 0.0) / total
        all_w[k, z] = (post * (precs[k] * ctfs[k])).astype(jnp.bfloat16)

        @pl.when(z < Z - 1)
        def _():
            w_go(k, z, True).start()

        @pl.when(z > 0)
        def _():
            w_go(k, z, False).start()

    for k in range(K):
        late = [h for h in range(H) if (k, h) not in early]
        for h in range(H):
            if h in late or k == 0:
                gather(k, h)
        gathered(k)
        scores(k)
        if k + 1 < K:
            for h in range(H):
                if (k + 1, h) not in early:
                    send_a(k + 1, h)
            for h in range(H):
                if (k + 1, h) in early:
                    gather(k + 1, h)
            weights(k)

    def b_block(zz, slot):
        return all_p.at[zz, :, slot]

    def b_forward(zz):
        out = []
        for dx in range(1, X):
            xx, cc = xc(dx, 0)
            out.append((g_send.at[zz, dx - 1, 0], dev(z, xx, cc)))
        for dc in range(1, C):
            xx, cc = xc(0, dc)
            out.append((g_send.at[zz, X - 1, dc - 1], dev(z, xx, cc)))
        return [
            pltpu.make_async_remote_copy(
                src_ref=b_block(zz, s), dst_ref=b_block(zz, s), send_sem=sem, recv_sem=b_recv.at[zz, s],
                device_id=to, device_id_type=MESH,
            )
            for sem, to in out
        ]

    def b_second(zz):
        out = []
        for dx in range(1, X):
            xx, _ = xc(dx, 0)
            slot = xx * C + c
            for dc in range(1, C):
                _, cc = xc(0, dc)
                out.append(pltpu.make_async_remote_copy(
                    src_ref=b_block(zz, slot), dst_ref=b_block(zz, slot), send_sem=g_send.at[zz, dx - 1, dc],
                    recv_sem=b_recv.at[zz, slot], device_id=dev(z, x, cc), device_id_type=MESH,
                ))
        return out

    def both(d, fn):
        @pl.when(z - d >= 0)
        def _():
            fn(z - d, True)

        @pl.when(z + d < Z)
        def _():
            fn(z + d, False)

    def b_start(zz, right):
        arrive(b_block(zz, s), b_recv.at[zz, s])
        for cp in b_forward(zz):
            cp.start()

    @pl.loop(1, Z)
    def _(d):
        both(d, b_start)

    weights(K - 1)

    def product(zz):
        w = jnp.concatenate([all_w[k, zz] for k in range(K)], axis=1)
        p = all_p[zz].reshape(K * nb, pb)
        return jnp.dot(w, p, preferred_element_type=jnp.float32)

    for cp in p_copies:
        cp.wait()
    sums_ref[...] = product(z)

    def w_step(src, right):
        for k in range(K):
            arrive(all_w.at[k, src], w_recv.at[k, src])

            @pl.when((z < Z - 1) if right else (z > 0))
            def _():
                w_go(k, src, right).start()

    def p_step(src, right):
        for dx in range(1, X):
            xx, _ = xc(dx, 0)
            arrive(b_block(src, xx * C + c), b_recv.at[src, xx * C + c])
        for cp in b_second(src):
            cp.start()

    def add_step(src, right):
        for dx in range(X):
            for dc in range(1, C):
                xx, cc = xc(dx, dc)
                arrive(b_block(src, xx * C + cc), b_recv.at[src, xx * C + cc])
        sums_ref[...] += product(src)

    @pl.loop(1, Z + 1)
    def _(d):
        both(d, w_step)
        both(d, p_step)

        @pl.when(d > 1)
        def _():
            both(d - 1, add_step)

    for cp in started:
        cp.wait_send()

    def end_step(src, right):
        for cp in b_forward(src) + b_second(src):
            cp.wait_send()

    @pl.loop(1, Z)
    def _(d):
        both(d, end_step)

    for k in range(K):
        @pl.loop(0, Z)
        def _(d):
            @pl.when((z - d >= 0) & (z < Z - 1))
            def _():
                w_go(k, z - d, True).wait_send()

            @pl.when((z + d < Z) & (z > 0))
            def _():
                w_go(k, z + d, False).wait_send()


def exchange(mesh, images, templates, group_ids, group_ctf, group_prec, log_prior, class_mask):
    Z, X, C, K = mesh.shape["img"], mesh.shape["tpl"], mesh.shape["sub"], CHUNKS
    S = X * C
    rows, pix = images.shape
    refs = templates.shape[0]
    r = rows // K
    nb = S * r
    pb = pix // Z
    H = 2 if r % 32 == 0 else 1
    vmem = pl.BlockSpec(memory_space=pltpu.VMEM)
    anyw = pl.BlockSpec(memory_space=pl.ANY)
    dma = pltpu.SemaphoreType.DMA
    f32, bf16 = jnp.float32, jnp.bfloat16
    class_sums, evid = pl.pallas_call(
        functools.partial(exchange_kernel, (Z, X, C, K, H)),
        out_shape=(
            pltpu.VMEM((refs, pb), f32),
            pltpu.VMEM((1, rows), f32),
        ),
        in_specs=[anyw] * 7,
        out_specs=(vmem, vmem),
        scratch_shapes=[
            pltpu.VMEM((1, S * rows), jnp.int32),
            pltpu.SMEM(group_ctf.shape, f32),
            pltpu.SMEM(group_prec.shape, f32),
            pltpu.SMEM(log_prior.shape, f32),
            pltpu.SMEM(class_mask.shape, jnp.int32),
            pltpu.VMEM((K, S, r, pix), bf16),
            pltpu.VMEM((refs, pix), bf16),
            pltpu.VMEM((refs, nb), f32),
            pltpu.VMEM((refs, nb), f32),
            pltpu.VMEM((refs, nb), f32),
            pltpu.VMEM((K, refs, nb), f32),
            pltpu.VMEM((K, Z, refs, nb), bf16),
            pltpu.VMEM((Z, K, S, r, pb), bf16),
            pltpu.VMEM((K, 8, nb), f32),
            pltpu.VMEM((K, S, 8, nb), f32),
            dma(()), dma((K,)), dma((K, H, S)), dma((K, H, S)), dma((K, H, max(X - 1, 1), max(C - 1, 1))),
            dma((max(Z - 1, 1),)), dma((Z, S)), dma((Z, X, C)), dma((K, max(S - 1, 1))), dma((K, S)),
            dma((2, K, Z)), dma((K, Z)), dma((K,)), dma((5,)),
        ],
        compiler_params=pltpu.CompilerParams(
            collective_id=0, has_side_effects=True, vmem_limit_bytes=56 * 1024 * 1024
        ),
    )(group_ids.reshape(1, S * rows), group_ctf, group_prec, log_prior, class_mask, images.reshape(K, r, pix), templates)
    return class_sums, evid.reshape(rows)


def solution(mesh):
    placed = (
        P(("groups", "img", "tpl", "sub"), None),
        P(("groups", "tpl", "sub"), None),
        P(("groups", "img")),
        P("groups"),
        P("groups"),
        P("groups"),
        P("groups"),
    )
    return jax.shard_map(
        functools.partial(exchange, mesh),
        mesh=mesh,
        in_specs=placed,
        out_specs=(P(("groups", "tpl", "sub"), "img"), P(("groups", "img", "tpl", "sub"))),
        check_vma=False,
    )
```

```python
import functools
import jax
import jax.numpy as jnp
from jax import lax
from jax.experimental import pallas as pl
from jax.experimental.pallas import tpu as pltpu
from jax.sharding import PartitionSpec as P

ROTS = 16
MASKED = -1e30
CHUNKS = 2
MESH = pl.DeviceIdType.MESH


def exchange_kernel(
    sizes, ids_in, ctf_in, prec_in, prior_in, mask_in, images, templates,
    sums_ref, evid_ref,
    ids_ref, ctf_ref, prec_ref, prior_ref, mask_ref, grid_buf, tmpl, tnorm, base, act, score, all_w, all_p, own_stat, stat,
    tmpl_sem, own_sem, a_send, a_recv, f_send, b_send, b_recv, g_send, s_send, s_recv,
    w_out, w_recv, p_own, in_sem,
):
    Z, X, C, K, H = sizes
    S = X * C
    g, z, x, c = [lax.axis_index(n) for n in ("groups", "img", "tpl", "sub")]
    s = x * C + c
    refs, nb = tnorm.shape
    classes = refs // ROTS
    r, pix = grid_buf.shape[2:]
    pb = pix // Z
    h_rows = r // H

    def xc(dx, dc):
        return lax.rem(x + dx, X), lax.rem(c + dc, C)

    def dev(zz, xx, cc):
        return (g, zz, xx, cc)

    def zoff(d):
        return lax.rem(z + d, Z)

    peers = [(dx, dc) for dx in range(X) for dc in range(C) if dx or dc]

    barrier = pltpu.get_barrier_semaphore()
    for dx, dc in peers:
        pl.semaphore_signal(barrier, inc=1, device_id=dev(z, *xc(dx, dc)), device_id_type=MESH)
    for d in range(1, Z):
        pl.semaphore_signal(barrier, inc=1, device_id=dev(zoff(d), x, c), device_id_type=MESH)

    started = []

    def local(src, dst, sem):
        cp = pltpu.make_async_copy(src, dst, sem)
        cp.start()
        return cp

    def remote(src, dst, send, recv, to):
        cp = pltpu.make_async_remote_copy(
            src_ref=src, dst_ref=dst, send_sem=send, recv_sem=recv, device_id=to, device_id_type=MESH
        )
        cp.start()
        started.append(cp)

    def arrive(dst, sem):
        pltpu.make_async_copy(dst, dst, sem).wait()

    small = [
        local(src, dst, in_sem.at[i])
        for i, (src, dst) in enumerate((
            (ids_in, ids_ref), (ctf_in, ctf_ref), (prec_in, prec_ref), (prior_in, prior_ref), (mask_in, mask_ref),
        ))
    ]
    tmpl_copy = local(templates, tmpl, tmpl_sem)
    own_copies = [local(images.at[k], grid_buf.at[k, s], own_sem.at[k]) for k in range(K)]

    pl.semaphore_wait(barrier, S - 1 + Z - 1)

    def piece(k, h, slot):
        return grid_buf.at[k, slot, pl.ds(h * h_rows, h_rows), :]

    def send_a(k, h):
        src = images.at[k, pl.ds(h * h_rows, h_rows), :]
        for dx in range(1, X):
            xx, cc = xc(dx, 0)
            remote(src, piece(k, h, s), a_send.at[k, h, dx - 1], a_recv.at[k, h, s], dev(z, xx, cc))
        for dc in range(1, C):
            xx, cc = xc(0, dc)
            remote(src, piece(k, h, s), a_send.at[k, h, X - 1 + dc - 1], a_recv.at[k, h, s], dev(z, xx, cc))

    order = [(k, h) for k in range(K) for h in range(H)]
    early = [(k, h) for k, h in order ]
    for k, h in early[:H]:
        send_a(k, h)
    for d in range(1, Z):
        zz = zoff(d)
        cols = pl.ds(pl.multiple_of(zz * pb, pb), pb)
        remote(images.at[:, :, cols], all_p.at[z, :, s], b_send.at[d - 1], b_recv.at[z, s], dev(zz, x, c))
    for k, h in early[H:]:
        send_a(k, h)

    for cp in small:
        cp.wait()
    first = s * classes
    for i in range(classes):
        rows = pl.ds(i * ROTS, ROTS)
        base[rows, :] = jnp.full((ROTS, nb), prior_ref[first + i], jnp.float32)
        act[rows, :] = jnp.full((ROTS, nb), mask_ref[first + i], jnp.int32).astype(jnp.float32)

    tmpl_copy.wait()

    @pl.loop(0, refs // 16)
    def _(i):
        rows = pl.ds(pl.multiple_of(i * 16, 16), 16)
        t = tmpl[rows, :].astype(jnp.float32)
        tnorm[rows, :] = jnp.broadcast_to(jnp.sum(t * t, axis=1, keepdims=True), (16, nb))

    all_ids = ids_ref[...]
    all_ctf = jnp.zeros(all_ids.shape, jnp.float32)
    all_prec = all_ctf
    for i in range(ctf_ref.shape[0]):
        hit = all_ids == i
        all_ctf = jnp.where(hit, ctf_ref[i], all_ctf)
        all_prec = jnp.where(hit, prec_ref[i], all_prec)

    def chunk(row, k):
        return jnp.concatenate([row[:, q * K * r + k * r : q * K * r + (k + 1) * r] for q in range(S)], axis=1)

    ctfs = [chunk(all_ctf, k) for k in range(K)]
    precs = [chunk(all_prec, k) for k in range(K)]

    def gather(k, h):
        for dx in range(1, X):
            xx, _ = xc(dx, 0)
            slot = xx * C + c
            arrive(piece(k, h, slot), a_recv.at[k, h, slot])
            for dc in range(1, C):
                _, cc = xc(0, dc)
                remote(piece(k, h, slot), piece(k, h, slot), f_send.at[k, h, dx - 1, dc - 1], a_recv.at[k, h, slot], dev(z, x, cc))

    def gathered(k):
        own_copies[k].wait()
        for h in range(H):
            for dx in range(X):
                for dc in range(1, C):
                    xx, cc = xc(dx, dc)
                    slot = xx * C + cc
                    arrive(piece(k, h, slot), a_recv.at[k, h, slot])

    p_copies = []

    def scores(k):
        pixels = grid_buf[k].reshape(nb, pix)
        raw = lax.dot_general(tmpl[...], pixels, (((1,), (1,)), ((), ())), preferred_element_type=jnp.float32)
        ctf, prec = ctfs[k], precs[k]
        values = (prec * ctf) * raw - (0.5 * prec * ctf * ctf) * tnorm[...] + base[...]
        values = jnp.where(act[...] > 0.0, values, MASKED)
        score[k] = values
        peak = jnp.max(values, axis=0, keepdims=True)
        total = jnp.sum(jnp.where(act[...] > 0.0, jnp.exp(values - peak), 0.0), axis=0, keepdims=True)
        row = lax.broadcasted_iota(jnp.int32, (8, nb), 0)
        own_stat[k] = jnp.where(row == 0, peak, total)
        for i, (dx, dc) in enumerate(peers):
            xx, cc = xc(dx, dc)
            remote(own_stat.at[k], stat.at[k, s], s_send.at[k, i], s_recv.at[k, s], dev(z, xx, cc))
        cols = pl.ds(pl.multiple_of(z * pb, pb), pb)
        p_copies.append(local(grid_buf.at[k, :, :, cols], all_p.at[z, k], p_own.at[k]))

    def w_go(k, zz, right):
        step = 1 if right else -1
        return pltpu.make_async_remote_copy(
            src_ref=all_w.at[k, zz], dst_ref=all_w.at[k, zz], send_sem=w_out.at[0 if right else 1, k, zz],
            recv_sem=w_recv.at[k, zz], device_id=dev(lax.rem(z + step + Z, Z), x, c), device_id_type=MESH,
        )

    def weights(k):
        parts = [(own_stat[k][0:1], own_stat[k][1:2])]
        for dx, dc in peers:
            xx, cc = xc(dx, dc)
            slot = xx * C + cc
            arrive(stat.at[k, slot], s_recv.at[k, slot])
            got = stat[k, slot]
            parts.append((got[0:1], got[1:2]))
        peak = functools.reduce(jnp.maximum, [p for p, _ in parts])
        total = functools.reduce(jnp.add, [t * jnp.exp(p - peak) for p, t in parts])
        evid = peak + jnp.log(total)
        mine = evid[:, 0:r]
        for q in range(1, S):
            mine = jnp.where(s == q, evid[:, q * r : (q + 1) * r], mine)
        evid_ref[:, k * r : (k + 1) * r] = mine
        post = jnp.where(act[...] > 0.0, jnp.exp(score[k] - peak), 0.0) / total
        all_w[k, z] = (post * (precs[k] * ctfs[k])).astype(jnp.bfloat16)

        @pl.when(z < Z - 1)
        def _():
            w_go(k, z, True).start()

        @pl.when(z > 0)
        def _():
            w_go(k, z, False).start()

    for k in range(K):
        late = [h for h in range(H) if (k, h) not in early]
        for h in range(H):
            if h in late or k == 0:
                gather(k, h)
        gathered(k)
        scores(k)
        if k + 1 < K:
            for h in range(H):
                if (k + 1, h) not in early:
                    send_a(k + 1, h)
            for h in range(H):
                if (k + 1, h) in early:
                    gather(k + 1, h)
            weights(k)

    def b_block(zz, slot):
        return all_p.at[zz, :, slot]

    def b_forward(zz):
        out = []
        for dx in range(1, X):
            xx, cc = xc(dx, 0)
            out.append((g_send.at[zz, dx - 1, 0], dev(z, xx, cc)))
        for dc in range(1, C):
            xx, cc = xc(0, dc)
            out.append((g_send.at[zz, X - 1, dc - 1], dev(z, xx, cc)))
        return [
            pltpu.make_async_remote_copy(
                src_ref=b_block(zz, s), dst_ref=b_block(zz, s), send_sem=sem, recv_sem=b_recv.at[zz, s],
                device_id=to, device_id_type=MESH,
            )
            for sem, to in out
        ]

    def b_second(zz):
        out = []
        for dx in range(1, X):
            xx, _ = xc(dx, 0)
            slot = xx * C + c
            for dc in range(1, C):
                _, cc = xc(0, dc)
                out.append(pltpu.make_async_remote_copy(
                    src_ref=b_block(zz, slot), dst_ref=b_block(zz, slot), send_sem=g_send.at[zz, dx - 1, dc],
                    recv_sem=b_recv.at[zz, slot], device_id=dev(z, x, cc), device_id_type=MESH,
                ))
        return out

    def both(d, fn):
        @pl.when(z - d >= 0)
        def _():
            fn(z - d, True)

        @pl.when(z + d < Z)
        def _():
            fn(z + d, False)

    def b_start(zz, right):
        arrive(b_block(zz, s), b_recv.at[zz, s])
        for cp in b_forward(zz):
            cp.start()

    @pl.loop(1, Z)
    def _(d):
        both(d, b_start)

    weights(K - 1)

    def product(zz):
        w = jnp.concatenate([all_w[k, zz] for k in range(K)], axis=1)
        p = all_p[zz].reshape(K * nb, pb)
        return jnp.dot(w, p, preferred_element_type=jnp.float32)

    for cp in p_copies:
        cp.wait()
    sums_ref[...] = product(z)

    def w_step(src, right):
        for k in range(K):
            arrive(all_w.at[k, src], w_recv.at[k, src])

            @pl.when((z < Z - 1) if right else (z > 0))
            def _():
                w_go(k, src, right).start()

    def p_step(src, right):
        for dx in range(1, X):
            xx, _ = xc(dx, 0)
            arrive(b_block(src, xx * C + c), b_recv.at[src, xx * C + c])
        for cp in b_second(src):
            cp.start()

    def add_step(src, right):
        for dx in range(X):
            for dc in range(1, C):
                xx, cc = xc(dx, dc)
                arrive(b_block(src, xx * C + cc), b_recv.at[src, xx * C + cc])
        sums_ref[...] += product(src)

    @pl.loop(1, Z + 1)
    def _(d):
        both(d, w_step)
        both(d, p_step)

        @pl.when(d > 1)
        def _():
            both(d - 1, add_step)

    for cp in started:
        cp.wait_send()

    def end_step(src, right):
        for cp in b_forward(src) + b_second(src):
            cp.wait_send()

    @pl.loop(1, Z)
    def _(d):
        both(d, end_step)

    for k in range(K):
        @pl.loop(0, Z)
        def _(d):
            @pl.when((z - d >= 0) & (z < Z - 1))
            def _():
                w_go(k, z - d, True).wait_send()

            @pl.when((z + d < Z) & (z > 0))
            def _():
                w_go(k, z + d, False).wait_send()


def exchange(mesh, images, templates, group_ids, group_ctf, group_prec, log_prior, class_mask):
    Z, X, C, K = mesh.shape["img"], mesh.shape["tpl"], mesh.shape["sub"], CHUNKS
    S = X * C
    rows, pix = images.shape
    refs = templates.shape[0]
    r = rows // K
    nb = S * r
    pb = pix // Z
    H = 2 if r % 32 == 0 else 1
    vmem = pl.BlockSpec(memory_space=pltpu.VMEM)
    anyw = pl.BlockSpec(memory_space=pl.ANY)
    dma = pltpu.SemaphoreType.DMA
    f32, bf16 = jnp.float32, jnp.bfloat16
    class_sums, evid = pl.pallas_call(
        functools.partial(exchange_kernel, (Z, X, C, K, H)),
        out_shape=(
            pltpu.VMEM((refs, pb), f32),
            pltpu.VMEM((1, rows), f32),
        ),
        in_specs=[anyw] * 7,
        out_specs=(vmem, vmem),
        scratch_shapes=[
            pltpu.VMEM((1, S * rows), jnp.int32),
            pltpu.SMEM(group_ctf.shape, f32),
            pltpu.SMEM(group_prec.shape, f32),
            pltpu.SMEM(log_prior.shape, f32),
            pltpu.SMEM(class_mask.shape, jnp.int32),
            pltpu.VMEM((K, S, r, pix), bf16),
            pltpu.VMEM((refs, pix), bf16),
            pltpu.VMEM((refs, nb), f32),
            pltpu.VMEM((refs, nb), f32),
            pltpu.VMEM((refs, nb), f32),
            pltpu.VMEM((K, refs, nb), f32),
            pltpu.VMEM((K, Z, refs, nb), bf16),
            pltpu.VMEM((Z, K, S, r, pb), bf16),
            pltpu.VMEM((K, 8, nb), f32),
            pltpu.VMEM((K, S, 8, nb), f32),
            dma(()), dma((K,)), dma((K, H, S)), dma((K, H, S)), dma((K, H, max(X - 1, 1), max(C - 1, 1))),
            dma((max(Z - 1, 1),)), dma((Z, S)), dma((Z, X, C)), dma((K, max(S - 1, 1))), dma((K, S)),
            dma((2, K, Z)), dma((K, Z)), dma((K,)), dma((5,)),
        ],
        compiler_params=pltpu.CompilerParams(
            collective_id=0, has_side_effects=True, vmem_limit_bytes=56 * 1024 * 1024
        ),
    )(group_ids.reshape(1, S * rows), group_ctf, group_prec, log_prior, class_mask, images.reshape(K, r, pix), templates)
    return class_sums, evid.reshape(rows)


def solution(mesh):
    placed = (
        P(("groups", "img", "tpl", "sub"), None),
        P(("groups", "tpl", "sub"), None),
        P(("groups", "img")),
        P("groups"),
        P("groups"),
        P("groups"),
        P("groups"),
    )
    return jax.shard_map(
        functools.partial(exchange, mesh),
        mesh=mesh,
        in_specs=placed,
        out_specs=(P(("groups", "tpl", "sub"), "img"), P(("groups", "img", "tpl", "sub"))),
        check_vma=False,
    )
```

```python
import functools
import jax
import jax.numpy as jnp
from jax import lax
from jax.experimental import pallas as pl
from jax.experimental.pallas import tpu as pltpu
from jax.sharding import PartitionSpec as P

ROTS = 16
MASKED = -1e30
CHUNKS = 2
MESH = pl.DeviceIdType.MESH


def exchange_kernel(
    sizes, ids_in, ctf_in, prec_in, prior_in, mask_in, images, templates,
    sums_ref, evid_ref,
    ids_ref, ctf_ref, prec_ref, prior_ref, mask_ref, grid_buf, tmpl, tnorm, base, act, score, all_w, all_p, own_stat, stat,
    tmpl_sem, own_sem, a_send, a_recv, f_send, b_send, b_recv, g_send, s_send, s_recv,
    w_out, w_recv, p_own, in_sem,
):
    Z, X, C, K, H = sizes
    S = X * C
    g, z, x, c = [lax.axis_index(n) for n in ("groups", "img", "tpl", "sub")]
    s = x * C + c
    refs, nb = tnorm.shape
    classes = refs // ROTS
    r, pix = grid_buf.shape[2:]
    pb = pix // Z
    h_rows = r // H

    def xc(dx, dc):
        return lax.rem(x + dx, X), lax.rem(c + dc, C)

    def dev(zz, xx, cc):
        return (g, zz, xx, cc)

    def zoff(d):
        return lax.rem(z + d, Z)

    peers = [(dx, dc) for dx in range(X) for dc in range(C) if dx or dc]

    barrier = pltpu.get_barrier_semaphore()
    for dx, dc in peers:
        pl.semaphore_signal(barrier, inc=1, device_id=dev(z, *xc(dx, dc)), device_id_type=MESH)
    for d in range(1, Z):
        pl.semaphore_signal(barrier, inc=1, device_id=dev(zoff(d), x, c), device_id_type=MESH)

    started = []

    def local(src, dst, sem):
        cp = pltpu.make_async_copy(src, dst, sem)
        cp.start()
        return cp

    def remote(src, dst, send, recv, to):
        cp = pltpu.make_async_remote_copy(
            src_ref=src, dst_ref=dst, send_sem=send, recv_sem=recv, device_id=to, device_id_type=MESH
        )
        cp.start()
        started.append(cp)

    def arrive(dst, sem):
        pltpu.make_async_copy(dst, dst, sem).wait()

    small = [
        local(src, dst, in_sem.at[i])
        for i, (src, dst) in enumerate((
            (ids_in, ids_ref), (ctf_in, ctf_ref), (prec_in, prec_ref), (prior_in, prior_ref), (mask_in, mask_ref),
        ))
    ]
    tmpl_copy = local(templates, tmpl, tmpl_sem)
    own_copies = [local(images.at[k], grid_buf.at[k, s], own_sem.at[k]) for k in range(K)]

    pl.semaphore_wait(barrier, S - 1 + Z - 1)

    def piece(k, h, slot):
        return grid_buf.at[k, slot, pl.ds(h * h_rows, h_rows), :]

    def send_a(k, h):
        src = images.at[k, pl.ds(h * h_rows, h_rows), :]
        for dx in range(1, X):
            xx, cc = xc(dx, 0)
            remote(src, piece(k, h, s), a_send.at[k, h, dx - 1], a_recv.at[k, h, s], dev(z, xx, cc))
        for dc in range(1, C):
            xx, cc = xc(0, dc)
            remote(src, piece(k, h, s), a_send.at[k, h, X - 1 + dc - 1], a_recv.at[k, h, s], dev(z, xx, cc))

    order = [(k, h) for k in range(K) for h in range(H)]
    early = [(k, h) for k, h in order ]
    for k, h in early[:H]:
        send_a(k, h)
    for d in range(1, Z):
        zz = zoff(d)
        cols = pl.ds(pl.multiple_of(zz * pb, pb), pb)
        remote(images.at[:, :, cols], all_p.at[z, :, s], b_send.at[d - 1], b_recv.at[z, s], dev(zz, x, c))
    for k, h in early[H:]:
        send_a(k, h)

    for cp in small:
        cp.wait()
    first = s * classes
    for i in range(classes):
        rows = pl.ds(i * ROTS, ROTS)
        base[rows, :] = jnp.full((ROTS, nb), prior_ref[first + i], jnp.float32)
        act[rows, :] = jnp.full((ROTS, nb), mask_ref[first + i], jnp.int32).astype(jnp.float32)

    tmpl_copy.wait()

    @pl.loop(0, refs // 16)
    def _(i):
        rows = pl.ds(pl.multiple_of(i * 16, 16), 16)
        t = tmpl[rows, :].astype(jnp.float32)
        tnorm[rows, :] = jnp.broadcast_to(jnp.sum(t * t, axis=1, keepdims=True), (16, nb))

    all_ids = ids_ref[...]
    all_ctf = jnp.zeros(all_ids.shape, jnp.float32)
    all_prec = all_ctf
    for i in range(ctf_ref.shape[0]):
        hit = all_ids == i
        all_ctf = jnp.where(hit, ctf_ref[i], all_ctf)
        all_prec = jnp.where(hit, prec_ref[i], all_prec)

    def chunk(row, k):
        return jnp.concatenate([row[:, q * K * r + k * r : q * K * r + (k + 1) * r] for q in range(S)], axis=1)

    ctfs = [chunk(all_ctf, k) for k in range(K)]
    precs = [chunk(all_prec, k) for k in range(K)]

    def gather(k, h):
        for dx in range(1, X):
            xx, _ = xc(dx, 0)
            slot = xx * C + c
            arrive(piece(k, h, slot), a_recv.at[k, h, slot])
            for dc in range(1, C):
                _, cc = xc(0, dc)
                remote(piece(k, h, slot), piece(k, h, slot), f_send.at[k, h, dx - 1, dc - 1], a_recv.at[k, h, slot], dev(z, x, cc))

    def gathered(k):
        own_copies[k].wait()
        for h in range(H):
            for dx in range(X):
                for dc in range(1, C):
                    xx, cc = xc(dx, dc)
                    slot = xx * C + cc
                    arrive(piece(k, h, slot), a_recv.at[k, h, slot])

    p_copies = []

    def scores(k):
        pixels = grid_buf[k].reshape(nb, pix)
        raw = lax.dot_general(tmpl[...], pixels, (((1,), (1,)), ((), ())), preferred_element_type=jnp.float32)
        ctf, prec = ctfs[k], precs[k]
        values = (prec * ctf) * raw - (0.5 * prec * ctf * ctf) * tnorm[...] + base[...]
        values = jnp.where(act[...] > 0.0, values, MASKED)
        score[k] = values
        peak = jnp.max(values, axis=0, keepdims=True)
        total = jnp.sum(jnp.where(act[...] > 0.0, jnp.exp(values - peak), 0.0), axis=0, keepdims=True)
        row = lax.broadcasted_iota(jnp.int32, (8, nb), 0)
        own_stat[k] = jnp.where(row == 0, peak, total)
        for i, (dx, dc) in enumerate(peers):
            xx, cc = xc(dx, dc)
            remote(own_stat.at[k], stat.at[k, s], s_send.at[k, i], s_recv.at[k, s], dev(z, xx, cc))
        cols = pl.ds(pl.multiple_of(z * pb, pb), pb)
        p_copies.append(local(grid_buf.at[k, :, :, cols], all_p.at[z, k], p_own.at[k]))

    def w_go(k, zz, right):
        step = 1 if right else -1
        return pltpu.make_async_remote_copy(
            src_ref=all_w.at[k, zz], dst_ref=all_w.at[k, zz], send_sem=w_out.at[0 if right else 1, k, zz],
            recv_sem=w_recv.at[k, zz], device_id=dev(lax.rem(z + step + Z, Z), x, c), device_id_type=MESH,
        )

    def weights(k):
        parts = [(own_stat[k][0:1], own_stat[k][1:2])]
        for dx, dc in peers:
            xx, cc = xc(dx, dc)
            slot = xx * C + cc
            arrive(stat.at[k, slot], s_recv.at[k, slot])
            got = stat[k, slot]
            parts.append((got[0:1], got[1:2]))
        peak = functools.reduce(jnp.maximum, [p for p, _ in parts])
        total = functools.reduce(jnp.add, [t * jnp.exp(p - peak) for p, t in parts])
        evid = peak + jnp.log(total)
        mine = evid[:, 0:r]
        for q in range(1, S):
            mine = jnp.where(s == q, evid[:, q * r : (q + 1) * r], mine)
        evid_ref[:, k * r : (k + 1) * r] = mine
        post = jnp.where(act[...] > 0.0, jnp.exp(score[k] - peak), 0.0) / total
        all_w[k, z] = (post * (precs[k] * ctfs[k])).astype(jnp.bfloat16)

        @pl.when(z < Z - 1)
        def _():
            w_go(k, z, True).start()

        @pl.when(z > 0)
        def _():
            w_go(k, z, False).start()

    for k in range(K):
        late = [h for h in range(H) if (k, h) not in early]
        for h in range(H):
            if h in late or k == 0:
                gather(k, h)
        gathered(k)
        scores(k)
        if k + 1 < K:
            for h in range(H):
                if (k + 1, h) not in early:
                    send_a(k + 1, h)
            for h in range(H):
                if (k + 1, h) in early:
                    gather(k + 1, h)
            weights(k)

    def b_block(zz, slot):
        return all_p.at[zz, :, slot]

    def b_forward(zz):
        out = []
        for dx in range(1, X):
            xx, cc = xc(dx, 0)
            out.append((g_send.at[zz, dx - 1, 0], dev(z, xx, cc)))
        for dc in range(1, C):
            xx, cc = xc(0, dc)
            out.append((g_send.at[zz, X - 1, dc - 1], dev(z, xx, cc)))
        return [
            pltpu.make_async_remote_copy(
                src_ref=b_block(zz, s), dst_ref=b_block(zz, s), send_sem=sem, recv_sem=b_recv.at[zz, s],
                device_id=to, device_id_type=MESH,
            )
            for sem, to in out
        ]

    def b_second(zz):
        out = []
        for dx in range(1, X):
            xx, _ = xc(dx, 0)
            slot = xx * C + c
            for dc in range(1, C):
                _, cc = xc(0, dc)
                out.append(pltpu.make_async_remote_copy(
                    src_ref=b_block(zz, slot), dst_ref=b_block(zz, slot), send_sem=g_send.at[zz, dx - 1, dc],
                    recv_sem=b_recv.at[zz, slot], device_id=dev(z, x, cc), device_id_type=MESH,
                ))
        return out

    def both(d, fn):
        @pl.when(z - d >= 0)
        def _():
            fn(z - d, True)

        @pl.when(z + d < Z)
        def _():
            fn(z + d, False)

    def b_start(zz, right):
        arrive(b_block(zz, s), b_recv.at[zz, s])
        for cp in b_forward(zz):
            cp.start()

    weights(K - 1)

    @pl.loop(1, Z)
    def _(d):
        both(d, b_start)

    def product(zz):
        w = jnp.concatenate([all_w[k, zz] for k in range(K)], axis=1)
        p = all_p[zz].reshape(K * nb, pb)
        return jnp.dot(w, p, preferred_element_type=jnp.float32)

    for cp in p_copies:
        cp.wait()
    sums_ref[...] = product(z)

    def w_step(src, right):
        for k in range(K):
            arrive(all_w.at[k, src], w_recv.at[k, src])

            @pl.when((z < Z - 1) if right else (z > 0))
            def _():
                w_go(k, src, right).start()

    def p_step(src, right):
        for dx in range(1, X):
            xx, _ = xc(dx, 0)
            arrive(b_block(src, xx * C + c), b_recv.at[src, xx * C + c])
        for cp in b_second(src):
            cp.start()

    def add_step(src, right):
        for dx in range(X):
            for dc in range(1, C):
                xx, cc = xc(dx, dc)
                arrive(b_block(src, xx * C + cc), b_recv.at[src, xx * C + cc])
        sums_ref[...] += product(src)

    @pl.loop(1, Z + 1)
    def _(d):
        both(d, w_step)
        both(d, p_step)

        @pl.when(d > 1)
        def _():
            both(d - 1, add_step)

    for cp in started:
        cp.wait_send()

    def end_step(src, right):
        for cp in b_forward(src) + b_second(src):
            cp.wait_send()

    @pl.loop(1, Z)
    def _(d):
        both(d, end_step)

    for k in range(K):
        @pl.loop(0, Z)
        def _(d):
            @pl.when((z - d >= 0) & (z < Z - 1))
            def _():
                w_go(k, z - d, True).wait_send()

            @pl.when((z + d < Z) & (z > 0))
            def _():
                w_go(k, z + d, False).wait_send()


def exchange(mesh, images, templates, group_ids, group_ctf, group_prec, log_prior, class_mask):
    Z, X, C, K = mesh.shape["img"], mesh.shape["tpl"], mesh.shape["sub"], CHUNKS
    S = X * C
    rows, pix = images.shape
    refs = templates.shape[0]
    r = rows // K
    nb = S * r
    pb = pix // Z
    H = 2 if r % 32 == 0 else 1
    vmem = pl.BlockSpec(memory_space=pltpu.VMEM)
    anyw = pl.BlockSpec(memory_space=pl.ANY)
    dma = pltpu.SemaphoreType.DMA
    f32, bf16 = jnp.float32, jnp.bfloat16
    class_sums, evid = pl.pallas_call(
        functools.partial(exchange_kernel, (Z, X, C, K, H)),
        out_shape=(
            pltpu.VMEM((refs, pb), f32),
            pltpu.VMEM((1, rows), f32),
        ),
        in_specs=[anyw] * 7,
        out_specs=(vmem, vmem),
        scratch_shapes=[
            pltpu.VMEM((1, S * rows), jnp.int32),
            pltpu.SMEM(group_ctf.shape, f32),
            pltpu.SMEM(group_prec.shape, f32),
            pltpu.SMEM(log_prior.shape, f32),
            pltpu.SMEM(class_mask.shape, jnp.int32),
            pltpu.VMEM((K, S, r, pix), bf16),
            pltpu.VMEM((refs, pix), bf16),
            pltpu.VMEM((refs, nb), f32),
            pltpu.VMEM((refs, nb), f32),
            pltpu.VMEM((refs, nb), f32),
            pltpu.VMEM((K, refs, nb), f32),
            pltpu.VMEM((K, Z, refs, nb), bf16),
            pltpu.VMEM((Z, K, S, r, pb), bf16),
            pltpu.VMEM((K, 8, nb), f32),
            pltpu.VMEM((K, S, 8, nb), f32),
            dma(()), dma((K,)), dma((K, H, S)), dma((K, H, S)), dma((K, H, max(X - 1, 1), max(C - 1, 1))),
            dma((max(Z - 1, 1),)), dma((Z, S)), dma((Z, X, C)), dma((K, max(S - 1, 1))), dma((K, S)),
            dma((2, K, Z)), dma((K, Z)), dma((K,)), dma((5,)),
        ],
        compiler_params=pltpu.CompilerParams(
            collective_id=0, has_side_effects=True, vmem_limit_bytes=56 * 1024 * 1024
        ),
    )(group_ids.reshape(1, S * rows), group_ctf, group_prec, log_prior, class_mask, images.reshape(K, r, pix), templates)
    return class_sums, evid.reshape(rows)


def solution(mesh):
    placed = (
        P(("groups", "img", "tpl", "sub"), None),
        P(("groups", "tpl", "sub"), None),
        P(("groups", "img")),
        P("groups"),
        P("groups"),
        P("groups"),
        P("groups"),
    )
    return jax.shard_map(
        functools.partial(exchange, mesh),
        mesh=mesh,
        in_specs=placed,
        out_specs=(P(("groups", "tpl", "sub"), "img"), P(("groups", "img", "tpl", "sub"))),
        check_vma=False,
    )
```
